32 devices in a mesh: dp: 8 (over y, x, core), tensor: 4 (over z).
Axes of the slice: x: 2, y: 2, z: 4, core: 2. Of those that a mesh axis runs over, the one named last changes fastest.
Arguments:
- tokens: bfloat16 [8192, 1024], P(('dp', 'tensor')), may hold values from -6 to 6
- cotangent: bfloat16 [8192, 1024], P(('dp', 'tensor')), may hold values from -6 to 6
- gain_attn: float32 [1024], replicated, may hold values from 0.5 to 1.5
- gain_ffn: float32 [1024], replicated, may hold values from 0.5 to 1.5
- w_query: bfloat16 [1024, 1024], P('dp', 'tensor'), may hold values from -0.1875 to 0.1875
- w_key: bfloat16 [1024, 1024], P('dp', 'tensor'), may hold values from -0.1875 to 0.1875
- w_value: bfloat16 [1024, 2048], P('dp', 'tensor'), may hold values from -0.1875 to 0.1875
- w_gate_out: bfloat16 [1024, 2048], P('dp', 'tensor'), may hold values from -0.1875 to 0.1875
- w_decay: bfloat16 [1024, 8], P('dp', 'tensor'), may hold values from -0.1875 to 0.1875
- w_beta: bfloat16 [1024, 8], P('dp', 'tensor'), may hold values from -0.1875 to 0.1875
- w_output: bfloat16 [2048, 1024], P('tensor', 'dp'), may hold values from -0.125 to 0.125
- w_ffn_gate: bfloat16 [1024, 2816], P('dp', 'tensor'), may hold values from -0.1875 to 0.1875
- w_ffn_up: bfloat16 [1024, 2816], P('dp', 'tensor'), may hold values from -0.1875 to 0.1875
- w_ffn_down: bfloat16 [2816, 1024], P('tensor', 'dp'), may hold values from -0.109375 to 0.109375
- conv_query: float32 [4, 1024], replicated, may hold values from -3 to 3
- conv_key: float32 [4, 1024], replicated, may hold values from -3 to 3
- conv_value: float32 [4, 2048], replicated, may hold values from -3 to 3
- a_log: float32 [8], replicated, may hold values from -2.5 to 1
- dt_bias: float32 [8], replicated, may hold values from -4 to -1
- out_gain: float32 [256], replicated, may hold values from 0.5 to 1.5
Outputs:
- output: bfloat16 [8192, 1024], P(('dp', 'tensor'))
- grad_tokens: float32 [8192, 1024], P(('dp', 'tensor'))
- grad_gain_attn: float32 [1024], replicated
- grad_gain_ffn: float32 [1024], replicated
- grad_w_query: float32 [1024, 1024], P('dp', 'tensor')
- grad_w_key: float32 [1024, 1024], P('dp', 'tensor')
- grad_w_value: float32 [1024, 2048], P('dp', 'tensor')
- grad_w_gate_out: float32 [1024, 2048], P('dp', 'tensor')
- grad_w_decay: float32 [1024, 8], P('dp', 'tensor')
- grad_w_beta: float32 [1024, 8], P('dp', 'tensor')
- grad_w_output: float32 [2048, 1024], P('tensor', 'dp')
- grad_w_ffn_gate: float32 [1024, 2816], P('dp', 'tensor')
- grad_w_ffn_up: float32 [1024, 2816], P('dp', 'tensor')
- grad_w_ffn_down: float32 [2816, 1024], P('tensor', 'dp')
- grad_conv_query: float32 [4, 1024], replicated
- grad_conv_key: float32 [4, 1024], replicated
- grad_conv_value: float32 [4, 2048], replicated
- grad_a_log: float32 [8], replicated
- grad_dt_bias: float32 [8], replicated
- grad_out_gain: float32 [256], replicated
The draws below stay inside these ranges and needn't reach their ends.
All inputs are finite; a program needn't handle non-finite values.
Results may differ from the reference program's by a relative error of at most 0.017.
Values may be sent and summed in bfloat16 or wider, within the bound.
No kernel may reach another device: no remote copies, remote signals or barrier semaphores. Data moves between devices by JAX's collectives and lax.ppermute only.
A program may use at most 192 MiB of HBM per device.

```python
import jax
import jax.numpy as jnp
from jax import lax

D = 1024
HEADS = 8
DK = 128
DV = 256
FF = 2816
CONV = 4
SPAN = 64
SEQ_LEN = 1024
HK = 1024
HV = 2048
GROUP_TOK = 1024
TOKENS = 8192
N_DP = 8


def level_of(rng, dims, cuts, least, top_value):
    def one(axis_at, parts):
        steps = jax.random.uniform(jax.random.fold_in(jax.random.fold_in(rng, 6), axis_at), (parts,), jnp.float32, least / len(cuts), top_value / len(cuts))
        return jnp.repeat(jnp.exp(steps), dims[axis_at] // parts).reshape((-1,) + (1,) * (len(dims) - axis_at - 1))

    factor_of = one(*cuts[0])
    for cut in cuts[1:]:
        factor_of = factor_of * one(*cut)
    return factor_of


def gaussian(stream_key, extent, deviation, limit, cuts=(), held_as=jnp.bfloat16):
    entries = deviation * jax.random.normal(stream_key, extent, jnp.float32)
    if cuts:
        entries = entries * level_of(stream_key, extent, cuts, -0.22, 0.18)
    return jnp.clip(entries, -limit, limit).astype(held_as)


def setup_inputs(seed: int = 0) -> dict:
    keys = jax.random.split(jax.random.key(seed), 21)
    return {
        "tokens": gaussian(keys[0], (TOKENS, D), 1.0, 6.0, ((0, 32),)),
        "cotangent": gaussian(keys[1], (TOKENS, D), 1.0, 6.0, ((0, 32),)),
        "gain_attn": jnp.clip(1.0 + 0.1 * jax.random.normal(keys[2], (D,), jnp.float32), 0.5, 1.5),
        "gain_ffn": jnp.clip(1.0 + 0.1 * jax.random.normal(keys[3], (D,), jnp.float32), 0.5, 1.5),
        "w_query": gaussian(keys[4], (D, HK), D ** -0.5, 0.1875, ((0, 8), (1, 4))),
        "w_key": gaussian(keys[5], (D, HK), D ** -0.5, 0.1875, ((0, 8), (1, 4))),
        "w_value": gaussian(keys[6], (D, HV), D ** -0.5, 0.1875, ((0, 8), (1, 4))),
        "w_gate_out": gaussian(keys[7], (D, HV), D ** -0.5, 0.1875, ((0, 8), (1, 4))),
        "w_decay": gaussian(keys[8], (D, HEADS), D ** -0.5, 0.1875, ((0, 8), (1, 4))),
        "w_beta": gaussian(keys[9], (D, HEADS), D ** -0.5, 0.1875, ((0, 8), (1, 4))),
        "w_output": gaussian(keys[10], (HV, D), HV ** -0.5, 0.125, ((0, 4), (1, 8))),
        "w_ffn_gate": gaussian(keys[11], (D, FF), D ** -0.5, 0.1875, ((0, 8), (1, 4))),
        "w_ffn_up": gaussian(keys[12], (D, FF), D ** -0.5, 0.1875, ((0, 8), (1, 4))),
        "w_ffn_down": gaussian(keys[13], (FF, D), FF ** -0.5, 0.109375, ((0, 4), (1, 8))),
        "conv_query": gaussian(keys[14], (CONV, HK), CONV ** -0.5, 3.0, (), jnp.float32),
        "conv_key": gaussian(keys[15], (CONV, HK), CONV ** -0.5, 3.0, (), jnp.float32),
        "conv_value": gaussian(keys[16], (CONV, HV), CONV ** -0.5, 3.0, (), jnp.float32),
        "a_log": jnp.clip(jax.random.uniform(keys[17], (HEADS,), jnp.float32, -2.5, 1.0), -2.5, 1.0),
        "dt_bias": jnp.clip(jax.random.uniform(keys[18], (HEADS,), jnp.float32, -4.0, -1.0), -4.0, -1.0),
        "out_gain": jnp.clip(1.0 + 0.1 * jax.random.normal(keys[19], (DV,), jnp.float32), 0.5, 1.5),
    }


@jax.custom_vjp
def low(v):
    return lax.optimization_barrier(v.astype(jnp.bfloat16)).astype(jnp.float32)

@jax.custom_vjp
def low_back(v):
    return v

def low_keep(v):
    return (low(v), None)

def low_pass(kept, grad):
    return (grad,)

def back_keep(v):
    return (v, None)

def back_low(kept, grad):
    return (low(grad),)
low.defvjp(low_keep, low_pass)
low_back.defvjp(back_keep, back_low)
PRECISE = lax.Precision.HIGHEST

def rms_norm(values, gain):
    return values * lax.rsqrt(lax.optimization_barrier(jnp.mean(values * values, -1, keepdims=True)) + 1e-05) * gain

def matmul_high(left, right):
    return jnp.dot(left, right, precision=PRECISE)

def conv_silu(pre_conv, taps):
    length = pre_conv.shape[1]
    padded = jnp.pad(pre_conv, ((0, 0), (CONV - 1, 0), (0, 0)))
    summed = padded[:, 0:length, :] * taps[0]
    for offset in range(1, CONV):
        summed = summed + padded[:, offset:offset + length, :] * taps[offset]
    return jax.nn.silu(summed)

def split_heads(values, width):
    seq_count = values.shape[0]
    return values.reshape(seq_count, SEQ_LEN // SPAN, SPAN, -1, width).transpose(0, 1, 3, 2, 4)

def per_head(values, seq_count):
    return values.reshape(seq_count, SEQ_LEN // SPAN, SPAN, -1).transpose(0, 1, 3, 2)

def span_step(carried, pieces):
    queries, key_rows, w_rows, u_rows, cumulative, inner_mix = pieces
    new_values = u_rows - jnp.einsum('shcd,shde->shce', w_rows, carried, precision=PRECISE)
    outcome = jnp.exp(cumulative)[..., None] * jnp.einsum('shcd,shde->shce', queries, carried, precision=PRECISE)
    outcome = outcome + jnp.einsum('shij,shje->shie', inner_mix, new_values, precision=PRECISE)
    final_log = cumulative[..., -1]
    weighted = key_rows * jnp.exp(final_log[..., None] - cumulative)[..., None]
    carried = jnp.exp(final_log)[..., None, None] * carried + jnp.einsum('shcd,shce->shde', weighted, new_values, precision=PRECISE)
    return (carried, outcome)

def delta_mixer(q_pre, k_pre, v_pre, o_pre, a_pre, b_pre, conv_q, conv_k, conv_v, a_log, dt_bias, out_gain):
    token_count = q_pre.shape[0]
    head_count = a_pre.shape[1]
    seq_count = token_count // SEQ_LEN
    queries = split_heads(conv_silu(q_pre.reshape(seq_count, SEQ_LEN, -1), conv_q), DK)
    queries = queries * lax.rsqrt(lax.optimization_barrier(jnp.sum(queries * queries, -1, keepdims=True)) + 1e-06) * DK ** (-0.5)
    key_rows = split_heads(conv_silu(k_pre.reshape(seq_count, SEQ_LEN, -1), conv_k), DK)
    key_rows = key_rows * lax.rsqrt(lax.optimization_barrier(jnp.sum(key_rows * key_rows, -1, keepdims=True)) + 1e-06)
    value_rows = split_heads(conv_silu(v_pre.reshape(seq_count, SEQ_LEN, -1), conv_v), DV)
    beta_rows = per_head(jax.nn.sigmoid(b_pre), seq_count)
    log_decay = per_head(-jnp.exp(a_log) * jax.nn.softplus(a_pre + dt_bias), seq_count)
    cumulative = jnp.cumsum(log_decay, axis=-1)
    row_ids = lax.broadcasted_iota(jnp.int32, (SPAN, SPAN), 0)
    col_ids = lax.broadcasted_iota(jnp.int32, (SPAN, SPAN), 1)
    causal = row_ids >= col_ids
    strict = (row_ids > col_ids).astype(jnp.float32)
    differ = cumulative[..., :, None] - cumulative[..., None, :]
    decays = jnp.exp(jnp.where(causal, differ, 0.0)) * causal.astype(jnp.float32)
    lower_mat = beta_rows[..., :, None] * jnp.einsum('snhid,snhjd->snhij', key_rows, key_rows, precision=PRECISE) * decays * strict
    identity = jnp.eye(SPAN, dtype=jnp.float32)
    inverse = identity - lower_mat
    powered = lower_mat
    for repeat in range(SPAN.bit_length() - 2):
        powered = jnp.einsum('snhij,snhjk->snhik', powered, powered, precision=PRECISE)
        inverse = jnp.einsum('snhij,snhjk->snhik', inverse, identity + powered, precision=PRECISE)
    w_rows = jnp.einsum('snhij,snhjd->snhid', inverse, (beta_rows * jnp.exp(cumulative))[..., None] * key_rows, precision=PRECISE)
    u_rows = jnp.einsum('snhij,snhjd->snhid', inverse, beta_rows[..., None] * value_rows, precision=PRECISE)
    inner_mix = jnp.einsum('snhid,snhjd->snhij', queries, key_rows, precision=PRECISE) * decays
    by_block = tuple((member.swapaxes(0, 1) for member in (queries, key_rows, w_rows, u_rows, cumulative, inner_mix)))
    start_state = jnp.zeros((seq_count, head_count, DK, DV), jnp.float32)
    final_state, outcome = lax.scan(jax.checkpoint(span_step), start_state, by_block)
    core_out = outcome.transpose(1, 0, 3, 2, 4).reshape(seq_count, SEQ_LEN, head_count, DV)
    gate_rows = o_pre.reshape(seq_count, SEQ_LEN, head_count, DV)
    normed = core_out * lax.rsqrt(lax.optimization_barrier(jnp.mean(core_out * core_out, -1, keepdims=True)) + 1e-05) * out_gain * jax.nn.silu(gate_rows)
    return normed.reshape(token_count, head_count * DV)

def forward(tok_rows, params):
    gain_attn, gain_ffn, w_query, w_key, w_value, w_gate_out, w_decay, w_beta, w_output, w_ffn_gate, w_ffn_up, w_ffn_down, conv_query, conv_key, conv_value, a_log, dt_bias, out_gain = params
    normed_one = low(rms_norm(tok_rows, gain_attn))
    q_pre = low_back(matmul_high(normed_one, w_query))
    k_pre = low_back(matmul_high(normed_one, w_key))
    v_pre = low_back(matmul_high(normed_one, w_value))
    o_pre = low_back(matmul_high(normed_one, w_gate_out))
    a_pre = low_back(matmul_high(normed_one, w_decay))
    b_pre = low_back(matmul_high(normed_one, w_beta))
    mixed = low(delta_mixer(q_pre, k_pre, v_pre, o_pre, a_pre, b_pre, conv_query, conv_key, conv_value, a_log, dt_bias, out_gain))
    branch = low_back(matmul_high(mixed, w_output))
    middle = tok_rows + branch
    normed_two = low(rms_norm(middle, gain_ffn))
    gate_val = low_back(matmul_high(normed_two, w_ffn_gate))
    up_val = low_back(matmul_high(normed_two, w_ffn_up))
    activated = low(jax.nn.silu(gate_val) * up_val)
    return middle + matmul_high(activated, w_ffn_down)

def reference(tokens, cotangent, gain_attn, gain_ffn, w_query, w_key, w_value, w_gate_out, w_decay, w_beta, w_output, w_ffn_gate, w_ffn_up, w_ffn_down, conv_query, conv_key, conv_value, a_log, dt_bias, out_gain):
    params = tuple((member.astype(jnp.float32) for member in (gain_attn, gain_ffn, w_query, w_key, w_value, w_gate_out, w_decay, w_beta, w_output, w_ffn_gate, w_ffn_up, w_ffn_down, conv_query, conv_key, conv_value, a_log, dt_bias, out_gain)))
    tok_blocks = tokens.astype(jnp.float32).reshape(N_DP, GROUP_TOK, D)
    cot_blocks = cotangent.astype(jnp.float32).reshape(N_DP, GROUP_TOK, D)

    def one_block(running, inputs):
        tok_block, cot_block = inputs
        outcome, pullback = jax.vjp(forward, tok_block, params)
        grad_block, grad_params = pullback(cot_block)
        return (jax.tree.map(jnp.add, running, grad_params), (outcome, grad_block))
    initial = jax.tree.map(jnp.zeros_like, params)
    totals, (outputs, grad_rows) = lax.scan(one_block, initial, (tok_blocks, cot_blocks))
    return (outputs.reshape(TOKENS, D).astype(jnp.bfloat16), grad_rows.reshape(TOKENS, D), totals[0], totals[1], totals[2], totals[3], totals[4], totals[5], totals[6], totals[7], totals[8], totals[9], totals[10], totals[11], totals[12], totals[13], totals[14], totals[15], totals[16], totals[17])
```

```python
import functools
import jax
import jax.numpy as jnp
from jax import lax
from jax.experimental import pallas as pl
from jax.experimental.pallas import tpu as pltpu
from jax.sharding import PartitionSpec as P

DK = 128
DV = 256
CONV = 4
SPAN = 64
SEQ_LEN = 1024
LANES = 128
F32 = jnp.float32
LOW = jnp.bfloat16


def mm(left, right, dims=((1,), (0,))):
    return lax.dot_general(
        left.astype(LOW), right.astype(LOW), (dims, ((), ())), preferred_element_type=F32
    )


NT = ((1,), (1,))
TN = ((0,), (0,))


def exact_dot(ones_mat, values):
    first = values.astype(LOW)
    rest = values - first.astype(F32)
    second = rest.astype(LOW)
    third = (rest - second.astype(F32)).astype(LOW)
    return mm(ones_mat, third) + mm(ones_mat, second) + mm(ones_mat, first)


def sigmoid(values):
    return 1.0 / (1.0 + jnp.exp(-values))


def softplus(values):
    return jnp.maximum(values, 0.0) + jnp.log1p(jnp.exp(-jnp.abs(values)))


def block_ones(rows, upper):
    row_ids = lax.broadcasted_iota(jnp.int32, (rows, rows), 0)
    col_ids = lax.broadcasted_iota(jnp.int32, (rows, rows), 1)
    same = (row_ids // SPAN) == (col_ids // SPAN)
    side = (row_ids <= col_ids) if upper else (row_ids >= col_ids)
    return jnp.where(same & side, 1.0, 0.0).astype(LOW)


def span_ids():
    return (
        lax.broadcasted_iota(jnp.int32, (SPAN, SPAN), 0),
        lax.broadcasted_iota(jnp.int32, (SPAN, SPAN), 1),
    )


def unit_lower_inverses(lowers):
    row_ids, col_ids = span_ids()
    inverses = None
    size = 1
    while size < SPAN:
        joined = (row_ids // (2 * size) == col_ids // (2 * size)) & (
            (row_ids // size) % 2 == 1
        ) & ((col_ids // size) % 2 == 0)
        parts = [jnp.where(joined, lower, 0.0) for lower in lowers]
        if inverses is None:
            eye = jnp.where(row_ids == col_ids, 1.0, 0.0)
            inverses = [eye - part for part in parts]
        else:
            halves = [mm(inverse, part) for inverse, part in zip(inverses, parts)]
            inverses = [
                inverse - mm(half, inverse) for half, inverse in zip(halves, inverses)
            ]
        size *= 2
    return inverses


class Columns:
    def __init__(self, head_count):
        self.q = 0
        self.k = head_count * DK
        self.v = 2 * head_count * DK
        self.o = self.v + head_count * DV
        self.ab = self.o + head_count * DV
        self.width = self.ab + LANES


def gates(ab_rows, par_ref, rows, head_count):
    shifted = ab_rows + par_ref[0:1, :]
    log_decay = -jnp.exp(par_ref[1:2, :]) * softplus(shifted)
    lane = lax.broadcasted_iota(jnp.int32, (rows, LANES), 1)
    log_decay = jnp.where(lane < head_count, log_decay, 0.0)
    cumulative = exact_dot(block_ones(rows, False), log_decay)
    beta = sigmoid(ab_rows)
    return shifted, log_decay, cumulative, beta


def conv_rows(padded, taps, start, cols):
    first = 8 - (CONV - 1) + start
    total = padded[first : first + SPAN, cols] * taps[0:1, :]
    for offset in range(1, CONV):
        total = total + padded[first + offset : first + offset + SPAN, cols] * taps[
            offset : offset + 1, :
        ]
    return total


def pair_inputs(head, block, cols, padded, taps_q, taps_k, taps_v, scal):
    cumulative, cum_t, beta, grow, fade = scal
    start = block * SPAN
    rows = slice(start, start + SPAN)
    qs = slice(cols.q + head * DK, cols.q + (head + 1) * DK)
    ks = slice(cols.k + head * DK, cols.k + (head + 1) * DK)
    vs = slice(cols.v + head * DV, cols.v + (head + 1) * DV)
    hk = slice(head * DK, (head + 1) * DK)
    hv = slice(head * DV, (head + 1) * DV)
    sq = conv_rows(padded, taps_q[:, hk], start, qs)
    sk = conv_rows(padded, taps_k[:, hk], start, ks)
    sv = conv_rows(padded, taps_v[:, hv], start, vs)
    gq, gk, gv = sigmoid(sq), sigmoid(sk), sigmoid(sv)
    cq, ck, cv = sq * gq, sk * gk, sv * gv
    rq = lax.rsqrt(jnp.sum(cq * cq, -1, keepdims=True) + 1e-06)
    rk = lax.rsqrt(jnp.sum(ck * ck, -1, keepdims=True) + 1e-06)
    unit_q = cq * rq
    key = ck * rk
    query = unit_q * DK ** (-0.5)
    cum_col = cumulative[rows, head : head + 1]
    cum_row = cum_t[head : head + 1, rows]
    row_ids, col_ids = span_ids()
    causal = row_ids >= col_ids
    decays = jnp.where(causal, jnp.exp(jnp.where(causal, cum_col - cum_row, 0.0)), 0.0)
    beta_col = beta[rows, head_lane(head, taps_q) : head_lane(head, taps_q) + 1]
    grow_col = grow[rows, head : head + 1]
    fade_col = fade[rows, head : head + 1]
    return dict(
        sq=sq, sk=sk, sv=sv, gq=gq, gk=gk, gv=gv, rq=rq, rk=rk, unit_q=unit_q, key=key,
        query=query, value=cv, decays=decays, beta=beta_col, grow=grow_col, fade=fade_col,
        strict=row_ids > col_ids,
    )


def head_lane(head, taps_q):
    return taps_q.shape[1] // DK + head


def chunk_scalars(ab_rows, par_ref, rows, head_count):
    shifted, log_decay, cumulative, beta = gates(ab_rows, par_ref, rows, head_count)
    cum_t = cumulative.T
    grow = jnp.exp(cumulative)
    fades = []
    ends = []
    for block in range(rows // SPAN):
        last = cumulative[(block + 1) * SPAN - 1 : (block + 1) * SPAN, :]
        fades.append(jnp.exp(last - cumulative[block * SPAN : (block + 1) * SPAN, :]))
        ends.append(jnp.exp(last))
    fade = jnp.concatenate(fades, 0) if len(fades) > 1 else fades[0]
    return shifted, log_decay, (cumulative, cum_t, beta, grow, fade), ends


def forward_kernel(
    head_count, rows, rank_ref, pre_ref, tq_ref, tk_ref, tv_ref, par_ref, gain_ref,
    mixed_ref, core_ref, state_ref, newv_ref, inv_ref, wrow_ref, carried, padded,
):
    cols = Columns(head_count)
    blocks = rows // SPAN
    conv_width = cols.o

    @pl.when(pl.program_id(1) == 0)
    def _():
        carried[...] = jnp.zeros_like(carried)
        padded[0:8, :] = jnp.zeros((8, conv_width), F32)

    @pl.when(pl.program_id(1) > 0)
    def _():
        padded[0:8, :] = padded[rows : rows + 8, :]

    padded[8 : 8 + rows, :] = pre_ref[:, 0:conv_width]
    _, _, scal, ends = chunk_scalars(
        pre_ref[:, cols.ab : cols.ab + LANES], par_ref, rows, head_count
    )
    taps = (tq_ref[...], tk_ref[...], tv_ref[...])
    pairs = [(block, head) for block in range(blocks) for head in range(head_count)]
    inputs, inners, lowers = [], [], []
    for block, head in pairs:
        got = pair_inputs(head, block, cols, padded, *taps, scal)
        both = jnp.concatenate([got["query"].astype(LOW), got["key"].astype(LOW)], 0)
        products = mm(both, got["key"], NT)
        inners.append((products[0:SPAN] * got["decays"]).astype(LOW))
        lowers.append(
            jnp.where(got["strict"], products[SPAN:] * got["decays"] * got["beta"], 0.0)
        )
        scaled = jnp.concatenate(
            [
                (got["beta"] * got["grow"] * got["key"]).astype(LOW),
                (got["beta"] * got["value"]).astype(LOW),
            ],
            1,
        )
        inputs.append(
            (
                scaled,
                (got["grow"] * got["query"]).astype(LOW),
                (got["fade"] * got["key"]).astype(LOW),
            )
        )
    ready = {}
    for (block, head), inverse, (scaled, read, faded), inner in zip(
        pairs, unit_lower_inverses(lowers), inputs, inners
    ):
        span = slice(block * SPAN, (block + 1) * SPAN)
        inverse = inverse.astype(LOW)
        inv_ref[span, head * SPAN : (head + 1) * SPAN] = inverse
        solved = mm(inverse, scaled)
        w_rows = solved[:, 0:DK].astype(LOW)
        wrow_ref[span, head * DK : (head + 1) * DK] = w_rows
        ready[block, head] = (
            jnp.concatenate([read, w_rows], 0), solved[:, DK:], inner, faded
        )
    states = [carried[head] for head in range(head_count)]
    for block in range(blocks):
        for head in range(head_count):
            state = states[head]
            sides, u_rows, inner, faded = ready[block, head]
            span = slice(block * SPAN, (block + 1) * SPAN)
            hv = slice(head * DV, (head + 1) * DV)
            low_state = state.astype(LOW)
            state_ref[0, block, head] = low_state
            read = mm(sides, low_state)
            new_values = (u_rows - read[SPAN:]).astype(LOW)
            newv_ref[span, hv] = new_values
            states[head] = ends[block][0:1, head : head + 1] * state + mm(faded, new_values, TN)
            core = read[0:SPAN] + mm(inner, new_values)
            core_ref[span, hv] = core.astype(LOW)
            gate = pre_ref[span, cols.o + head * DV : cols.o + (head + 1) * DV]
            scale = lax.rsqrt(jnp.mean(core * core, -1, keepdims=True) + 1e-05)
            mixed_ref[span, hv] = (
                core * scale * gain_ref[...] * (gate * sigmoid(gate))
            ).astype(LOW)
    for head in range(head_count):
        carried[head] = states[head]


def mixer_forward(pre, taps_q, taps_k, taps_v, params, gain, rank, head_count, rows=256):
    cols = Columns(head_count)
    tokens = pre.shape[0]
    seqs = tokens // SEQ_LEN
    chunks = SEQ_LEN // rows
    blocks = rows // SPAN
    kw, vw = head_count * DK, head_count * DV
    at = lambda s, c, rk: (s * chunks + c, 0)
    spec = pltpu.PrefetchScalarGridSpec(
        num_scalar_prefetch=1,
        grid=(seqs, chunks),
        in_specs=[
            pl.BlockSpec((rows, cols.width), at),
            pl.BlockSpec((CONV, kw), lambda s, c, rk: (0, rk[0])),
            pl.BlockSpec((CONV, kw), lambda s, c, rk: (0, rk[0])),
            pl.BlockSpec((CONV, vw), lambda s, c, rk: (0, rk[0])),
            pl.BlockSpec((8, LANES), lambda s, c, rk: (0, 0)),
            pl.BlockSpec((1, DV), lambda s, c, rk: (0, 0)),
        ],
        out_specs=[
            pl.BlockSpec((rows, vw), at),
            pl.BlockSpec((rows, vw), at),
            pl.BlockSpec((1, blocks, head_count, DK, DV), lambda s, c, rk: (s, c, 0, 0, 0)),
            pl.BlockSpec((rows, vw), at),
            pl.BlockSpec((rows, head_count * SPAN), at),
            pl.BlockSpec((rows, kw), at),
        ],
        scratch_shapes=[
            pltpu.VMEM((head_count, DK, DV), F32),
            pltpu.VMEM((rows + 8, cols.o), F32),
        ],
    )
    shape = jax.ShapeDtypeStruct
    return pl.pallas_call(
        functools.partial(forward_kernel, head_count, rows),
        grid_spec=spec,
        out_shape=[
            shape((tokens, vw), LOW),
            shape((tokens, vw), LOW),
            shape((seqs, SEQ_LEN // SPAN, head_count, DK, DV), LOW),
            shape((tokens, vw), LOW),
            shape((tokens, head_count * SPAN), LOW),
            shape((tokens, kw), LOW),
        ],
        compiler_params=pltpu.CompilerParams(
            dimension_semantics=("arbitrary", "arbitrary"), vmem_limit_bytes=48 * 1024 * 1024
        ),
        name="mixer_forward",
    )(rank, pre, taps_q, taps_k, taps_v, params, gain)


def backward_kernel(
    head_count, rows, rank_ref, pre_ref, prev_ref, tq_ref, tk_ref, tv_ref, par_ref, gain_ref,
    dmix_ref, core_ref, state_ref, newv_ref, inv_ref, wrow_ref,
    dpre_ref, dtaps_ref, dpar_ref, dgain_ref, carried, padded, dconv,
):
    cols = Columns(head_count)
    blocks = rows // SPAN
    conv_width = cols.o
    chunk = pl.num_programs(1) - 1 - pl.program_id(1)

    @pl.when((pl.program_id(0) == 0) & (pl.program_id(1) == 0))
    def _():
        dtaps_ref[...] = jnp.zeros_like(dtaps_ref)
        dpar_ref[...] = jnp.zeros_like(dpar_ref)
        dgain_ref[...] = jnp.zeros_like(dgain_ref)

    @pl.when(pl.program_id(1) == 0)
    def _():
        carried[...] = jnp.zeros_like(carried)
        dconv[rows : rows + 8, :] = jnp.zeros((8, conv_width), F32)

    @pl.when(pl.program_id(1) > 0)
    def _():
        dconv[rows : rows + 8, :] = dconv[0:8, :]

    padded[0:8, :] = jnp.where(chunk > 0, prev_ref[:, 0:conv_width], 0.0)
    padded[8 : 8 + rows, :] = pre_ref[:, 0:conv_width]
    shifted, log_decay, scal, ends = chunk_scalars(
        pre_ref[:, cols.ab : cols.ab + LANES], par_ref, rows, head_count
    )
    beta_all = scal[2]
    taps = (tq_ref[...], tk_ref[...], tv_ref[...])
    row_ids, col_ids = span_ids()
    upper_ones = jnp.where(row_ids <= col_ids, 1.0, 0.0).astype(LOW)
    gain = gain_ref[...]
    dgain = jnp.zeros((1, DV), F32)
    ready = {}
    for block in range(blocks):
        span = slice(block * SPAN, (block + 1) * SPAN)
        for head in range(head_count):
            hv = slice(head * DV, (head + 1) * DV)
            got = pair_inputs(head, block, cols, padded, *taps, scal)
            gate = pre_ref[span, cols.o + head * DV : cols.o + (head + 1) * DV]
            core = core_ref[span, hv].astype(F32)
            d_mixed = dmix_ref[span, hv].astype(F32)
            scale = lax.rsqrt(jnp.mean(core * core, -1, keepdims=True) + 1e-05)
            unit = core * scale
            sig_gate = sigmoid(gate)
            act_gate = gate * sig_gate
            with_unit = d_mixed * unit
            dgain = dgain + jnp.sum(with_unit * act_gate, 0, keepdims=True)
            dpre_ref[span, cols.o + head * DV : cols.o + (head + 1) * DV] = (
                with_unit * gain * (sig_gate + act_gate * (1.0 - sig_gate))
            ).astype(LOW)
            d_unit = d_mixed * gain * act_gate
            d_core = (
                scale * (d_unit - unit * jnp.mean(d_unit * unit, -1, keepdims=True))
            ).astype(LOW)
            query, key = got["query"].astype(LOW), got["key"].astype(LOW)
            both = jnp.concatenate([query, key], 0)
            products = mm(both, key, NT)
            got["inner"] = products[0:SPAN] * got["decays"]
            got["kk"] = jnp.where(got["strict"], products[SPAN:] * got["decays"], 0.0)
            got["both"] = both
            got["read"] = got["grow"] * got["query"]
            got["faded"] = got["fade"] * got["key"]
            got["d_core"] = d_core
            got["from_read"] = mm(got["read"], d_core, TN)
            got["from_inner"] = mm(got["inner"], d_core, TN)
            ready[block, head] = got
    dgain_ref[...] += dgain
    d_states = [carried[head] for head in range(head_count)]
    for block in reversed(range(blocks)):
        for head in range(head_count):
            d_state = d_states[head]
            span = slice(block * SPAN, (block + 1) * SPAN)
            hv = slice(head * DV, (head + 1) * DV)
            got = ready[block, head]
            low_d = d_state.astype(LOW)
            d_new = (got["from_inner"] + mm(got["faded"], low_d)).astype(LOW)
            w_rows = wrow_ref[span, head * DK : (head + 1) * DK]
            end = ends[block][0:1, head : head + 1]
            got["d_faded"] = mm(newv_ref[span, hv], low_d, NT)
            kept = end * d_state
            got["d_end"] = jnp.sum(
                jnp.sum(kept * state_ref[0, block, head].astype(F32), 0, keepdims=True),
                1,
                keepdims=True,
            )
            d_states[head] = got["from_read"] - mm(w_rows, d_new, TN) + kept
            got["d_new"] = d_new
    for head in range(head_count):
        carried[head] = d_states[head]
    lane = lax.broadcasted_iota(jnp.int32, (SPAN, LANES), 1)
    d_cums, d_betas = [], []
    for block in range(blocks):
        span = slice(block * SPAN, (block + 1) * SPAN)
        summed = jnp.zeros((SPAN, LANES), F32)
        direct = jnp.zeros((SPAN, LANES), F32)
        d_beta_all = jnp.zeros((SPAN, LANES), F32)
        for head in range(head_count):
            got = ready[block, head]
            hv = slice(head * DV, (head + 1) * DV)
            inverse = inv_ref[span, head * SPAN : (head + 1) * SPAN]
            solved = mm(inverse, got["d_new"], TN)
            left = jnp.concatenate([got["d_core"], solved.astype(LOW)], 0)
            right = jnp.concatenate([state_ref[0, block, head], newv_ref[span, hv]], 0)
            wide = mm(left, right, NT)
            d_read, d_inner = wide[0:SPAN, 0:DK], wide[0:SPAN, DK:]
            d_wk = -wide[SPAN:, 0:DK]
            d_lower = jnp.where(got["strict"], -wide[SPAN:, DK:], 0.0)
            beta, grow, fade, key = got["beta"], got["grow"], got["fade"], got["key"]
            grown = grow * key
            with_grown = jnp.sum(d_wk * grown, -1, keepdims=True)
            lower_kk = d_lower * got["kk"]
            crossing = beta * lower_kk + d_inner * got["inner"]
            tails = jnp.where(got["strict"], mm(upper_ones, crossing), 0.0)
            faded_sum = jnp.sum(got["d_faded"] * got["faded"], -1, keepdims=True)
            point = (
                jnp.sum(d_read * got["read"], -1, keepdims=True)
                - faded_sum
                + beta * with_grown
            )
            whole = (
                jnp.sum(tails, -1, keepdims=True)
                + got["d_end"]
                + jnp.sum(faded_sum, 0, keepdims=True)
            )
            d_beta = (
                with_grown
                + jnp.sum(solved * got["value"], -1, keepdims=True)
                + jnp.sum(lower_kk, -1, keepdims=True)
            )
            summed = jnp.where(lane == head, point, summed)
            direct = jnp.where(lane == head, whole, direct)
            d_beta_all = jnp.where(lane == head_count + head, d_beta, d_beta_all)
            d_qk = d_inner * got["decays"]
            d_kk = d_lower * got["decays"] * beta
            d_both = jnp.concatenate([d_qk.astype(LOW), d_kk.astype(LOW)], 0)
            forward_part = mm(d_both, got["both"][SPAN:])
            d_query = grow * d_read + forward_part[0:SPAN]
            d_key = (
                fade * got["d_faded"]
                + beta * grow * d_wk
                + forward_part[SPAN:]
                + mm(d_both, got["both"], TN)
            )
            d_unit_q = d_query * DK ** (-0.5)
            unit_q = got["unit_q"]
            d_cq = got["rq"] * (
                d_unit_q - unit_q * jnp.sum(d_unit_q * unit_q, -1, keepdims=True)
            )
            d_ck = got["rk"] * (d_key - key * jnp.sum(d_key * key, -1, keepdims=True))
            d_cv = beta * solved
            for d_act, pre_act, sig, first, size in (
                (d_cq, got["sq"], got["gq"], cols.q + head * DK, DK),
                (d_ck, got["sk"], got["gk"], cols.k + head * DK, DK),
                (d_cv, got["sv"], got["gv"], cols.v + head * DV, DV),
            ):
                dconv[span, first : first + size] = d_act * sig * (1.0 + pre_act * (1.0 - sig))
        d_cums.append((summed, direct))
        d_betas.append(d_beta_all)
    join = lambda parts: jnp.concatenate(parts, 0) if len(parts) > 1 else parts[0]
    d_log = exact_dot(block_ones(rows, True), join([p[0] for p in d_cums])) + join(
        [p[1] for p in d_cums]
    )
    lanes_all = lax.broadcasted_iota(jnp.int32, (rows, LANES), 1)
    d_a = jnp.where(
        lanes_all < head_count, d_log * -jnp.exp(par_ref[1:2, :]) * sigmoid(shifted), 0.0
    )
    d_b = join(d_betas) * beta_all * (1.0 - beta_all)
    dpre_ref[:, cols.ab : cols.ab + LANES] = (d_a + d_b).astype(LOW)
    dpar_ref[0:1, :] += jnp.sum(d_a, 0, keepdims=True)
    dpar_ref[1:2, :] += jnp.sum(d_log * log_decay, 0, keepdims=True)
    for taps_now, base in ((taps[0], cols.q), (taps[1], cols.k), (taps[2], cols.v)):
        width = taps_now.shape[1]
        for part in range(width // LANES):
            col = slice(base + part * LANES, base + (part + 1) * LANES)
            for block in range(blocks):
                start = block * SPAN
                total = None
                now = dconv[start : start + SPAN, col]
                for tap in range(CONV):
                    ahead = start + CONV - 1 - tap
                    tap_row = taps_now[tap : tap + 1, part * LANES : (part + 1) * LANES]
                    term = (now if tap == CONV - 1 else dconv[ahead : ahead + SPAN, col]) * tap_row
                    total = term if total is None else total + term
                    behind = 8 - (CONV - 1) + tap + start
                    dtaps_ref[tap : tap + 1, col] += jnp.sum(
                        now * padded[behind : behind + SPAN, col], 0, keepdims=True
                    )
                dpre_ref[start : start + SPAN, col] = total.astype(LOW)


def mixer_backward(pre, taps_q, taps_k, taps_v, params, gain, rank, d_mixed, saved, head_count,
                   rows=256):
    cols = Columns(head_count)
    tokens = pre.shape[0]
    seqs = tokens // SEQ_LEN
    chunks = SEQ_LEN // rows
    blocks = rows // SPAN
    kw, vw = head_count * DK, head_count * DV
    at = lambda s, c, rk: (s * chunks + chunks - 1 - c, 0)
    before = lambda s, c, rk: (
        jnp.maximum((s * chunks + chunks - 1 - c) * (rows // 8) - 1, 0), 0)
    fixed = lambda s, c, rk: (0, 0)
    spec = pltpu.PrefetchScalarGridSpec(
        num_scalar_prefetch=1,
        grid=(seqs, chunks),
        in_specs=[
            pl.BlockSpec((rows, cols.width), at),
            pl.BlockSpec((8, cols.width), before),
            pl.BlockSpec((CONV, kw), lambda s, c, rk: (0, rk[0])),
            pl.BlockSpec((CONV, kw), lambda s, c, rk: (0, rk[0])),
            pl.BlockSpec((CONV, vw), lambda s, c, rk: (0, rk[0])),
            pl.BlockSpec((8, LANES), fixed),
            pl.BlockSpec((1, DV), fixed),
            pl.BlockSpec((rows, vw), at),
            pl.BlockSpec((rows, vw), at),
            pl.BlockSpec((1, blocks, head_count, DK, DV),
                         lambda s, c, rk: (s, chunks - 1 - c, 0, 0, 0)),
            pl.BlockSpec((rows, vw), at),
            pl.BlockSpec((rows, head_count * SPAN), at),
            pl.BlockSpec((rows, kw), at),
        ],
        out_specs=[
            pl.BlockSpec((rows, cols.width), at),
            pl.BlockSpec((CONV, cols.o), fixed),
            pl.BlockSpec((8, LANES), fixed),
            pl.BlockSpec((1, DV), fixed),
        ],
        scratch_shapes=[
            pltpu.VMEM((head_count, DK, DV), F32),
            pltpu.VMEM((rows + 8, cols.o), F32),
            pltpu.VMEM((rows + 8, cols.o), F32),
        ],
    )
    shape = jax.ShapeDtypeStruct
    return pl.pallas_call(
        functools.partial(backward_kernel, head_count, rows),
        grid_spec=spec,
        out_shape=[
            shape((tokens, cols.width), LOW),
            shape((CONV, cols.o), F32),
            shape((8, LANES), F32),
            shape((1, DV), F32),
        ],
        compiler_params=pltpu.CompilerParams(
            dimension_semantics=("arbitrary", "arbitrary"), vmem_limit_bytes=48 * 1024 * 1024
        ),
        name="mixer_backward",
    )(rank, pre, pre, taps_q, taps_k, taps_v, params, gain, d_mixed, *saved)


def rms_norm(values, gain):
    return values * lax.rsqrt(jnp.mean(values * values, -1, keepdims=True) + 1e-05) * gain


def swiglu_act(gate_val, up_val):
    return jax.nn.silu(gate_val) * up_val


def matmul_tn(left, right):
    return lax.dot_general(left, right, (TN, ((), ())), preferred_element_type=F32)


def matmul_nt(left, right):
    return lax.dot_general(left, right, (NT, ((), ())), preferred_element_type=F32)


def place_cols(member, width, offset):
    blank = jnp.zeros(member.shape[:-1] + (width,), F32)
    return lax.dynamic_update_slice_in_dim(blank, member, offset, member.ndim - 1)


def head_params(a_log, dt_bias, rank, head_count):
    slab = jnp.zeros((8, LANES), F32)
    bias = lax.dynamic_slice_in_dim(dt_bias, rank * head_count, head_count, 0)
    scale = lax.dynamic_slice_in_dim(a_log, rank * head_count, head_count, 0)
    slab = lax.dynamic_update_slice(slab, bias[None, :], (0, 0))
    return lax.dynamic_update_slice(slab, scale[None, :], (1, 0))


def join_mixer_weights(w_query, w_key, w_value, w_gate_out, w_decay, w_beta):
    blank = jnp.zeros((w_query.shape[0], LANES - 2 * w_decay.shape[1]), LOW)
    return jnp.concatenate(
        [w_query, w_key, w_value, w_gate_out, w_decay, w_beta, blank], axis=1
    )


def local_general(
    tokens, cotangent, gain_attn, gain_ffn, w_query, w_key, w_value, w_gate_out, w_decay,
    w_beta, w_output, w_ffn_gate, w_ffn_up, w_ffn_down, conv_query, conv_key, conv_value,
    a_log, dt_bias, out_gain,
):
    rank = lax.axis_index("tensor")
    head_count = w_decay.shape[1]
    cols = Columns(head_count)
    gather_rows = lambda value: lax.all_gather(value, "dp", axis=0, tiled=True)
    gather_cols = lambda value: lax.all_gather(value, "dp", axis=1, tiled=True)
    gather_tokens = lambda value: lax.all_gather(value, "tensor", axis=0, tiled=True)
    mixer_weights = gather_rows(
        join_mixer_weights(w_query, w_key, w_value, w_gate_out, w_decay, w_beta)
    )
    output_weights = gather_cols(w_output)
    gate_weights, up_weights = gather_rows(w_ffn_gate), gather_rows(w_ffn_up)
    down_weights = gather_cols(w_ffn_down)

    def scatter_tokens(value):
        return lax.psum_scatter(
            value.astype(LOW), "tensor", scatter_dimension=0, tiled=True
        ).astype(F32)

    tok_rows = tokens.astype(F32)
    normed_one, norm_one_pull = jax.vjp(rms_norm, tok_rows, gain_attn)
    mixer_in = gather_tokens(normed_one.astype(LOW))
    pre = jnp.dot(mixer_in, mixer_weights, preferred_element_type=F32)
    kernel_args = (
        pre, conv_query, conv_key, conv_value,
        head_params(a_log, dt_bias, rank, head_count), out_gain.reshape(1, DV),
        rank.reshape(1).astype(jnp.int32),
    )
    mixed, *saved = mixer_forward(*kernel_args, head_count)
    middle = tok_rows + scatter_tokens(
        jnp.dot(mixed, output_weights, preferred_element_type=F32)
    )
    normed_two, norm_two_pull = jax.vjp(rms_norm, middle, gain_ffn)
    ffn_in = gather_tokens(normed_two.astype(LOW))
    gate_val = jnp.dot(ffn_in, gate_weights, preferred_element_type=F32)
    up_val = jnp.dot(ffn_in, up_weights, preferred_element_type=F32)
    activated, swiglu_pull = jax.vjp(swiglu_act, gate_val, up_val)
    activated_low = activated.astype(LOW)
    output = (
        middle
        + scatter_tokens(jnp.dot(activated_low, down_weights, preferred_element_type=F32))
    ).astype(LOW)
    cot_rows = gather_tokens(cotangent)
    d_gate, d_up = swiglu_pull(matmul_nt(cot_rows, down_weights))
    d_gate, d_up = d_gate.astype(LOW), d_up.astype(LOW)
    grad_down = matmul_tn(activated_low, cot_rows)
    grad_gate, grad_up = matmul_tn(ffn_in, d_gate), matmul_tn(ffn_in, d_up)
    d_normed_two = scatter_tokens(
        matmul_nt(d_gate, gate_weights) + matmul_nt(d_up, up_weights)
    )
    d_middle_norm, d_gain_ffn = norm_two_pull(d_normed_two)
    d_middle = cotangent.astype(F32) + d_middle_norm
    branch_cot = gather_tokens(d_middle.astype(LOW))
    d_mixed = matmul_nt(branch_cot, output_weights).astype(LOW)
    grad_out = matmul_tn(mixed, branch_cot)
    d_pre, d_taps, d_heads, d_out_gain = mixer_backward(*kernel_args, d_mixed, saved, head_count)
    grad_mixer = matmul_tn(mixer_in, d_pre)
    d_normed_one = scatter_tokens(matmul_nt(d_pre, mixer_weights))
    d_tok_norm, d_gain_attn = norm_one_pull(d_normed_one)
    grad_tokens = d_middle + d_tok_norm

    def scatter_grad(value, dim):
        return lax.psum_scatter(
            value.astype(LOW), "dp", scatter_dimension=dim, tiled=True
        ).astype(F32)

    own_mixer = scatter_grad(grad_mixer, 0)
    edge = cols.ab + head_count
    small_sums = lax.psum(
        (
            d_gain_attn,
            d_gain_ffn,
            place_cols(d_taps[:, : cols.k], conv_query.shape[1], rank * cols.k),
            place_cols(d_taps[:, cols.k : cols.v], conv_key.shape[1], rank * cols.k),
            place_cols(d_taps[:, cols.v :], conv_value.shape[1], rank * (cols.o - cols.v)),
            place_cols(d_heads[1, :head_count], a_log.shape[0], rank * head_count),
            place_cols(d_heads[0, :head_count], dt_bias.shape[0], rank * head_count),
            d_out_gain[0],
        ),
        ("dp", "tensor"),
    )
    return (
        output, grad_tokens, small_sums[0], small_sums[1],
        own_mixer[:, : cols.k], own_mixer[:, cols.k : cols.v], own_mixer[:, cols.v : cols.o],
        own_mixer[:, cols.o : cols.ab], own_mixer[:, cols.ab : edge],
        own_mixer[:, edge : edge + head_count],
        scatter_grad(grad_out, 1), scatter_grad(grad_gate, 0), scatter_grad(grad_up, 0),
        scatter_grad(grad_down, 1), *small_sums[2:],
    )


def solution(mesh):
    spread = P(("dp", "tensor"), None)
    rows_split, cols_split = P("dp", "tensor"), P("tensor", "dp")
    return jax.shard_map(
        local_general,
        mesh=mesh,
        in_specs=(spread, spread, P(), P())
        + (rows_split,) * 6
        + (cols_split, rows_split, rows_split, cols_split)
        + (P(),) * 6,
        out_specs=(spread, spread, P(), P())
        + (rows_split,) * 6
        + (cols_split, rows_split, rows_split, cols_split)
        + (P(),) * 6,
        check_vma=False,
    )
```

```python
import functools
import jax
import jax.numpy as jnp
from jax import lax
from jax.experimental import pallas as pl
from jax.experimental.pallas import tpu as pltpu
from jax.sharding import PartitionSpec as P

DK = 128
DV = 256
CONV = 4
SPAN = 64
SEQ_LEN = 1024
LANES = 128
F32 = jnp.float32
LOW = jnp.bfloat16


def mm(left, right, dims=((1,), (0,))):
    return lax.dot_general(
        left.astype(LOW), right.astype(LOW), (dims, ((), ())), preferred_element_type=F32
    )


NT = ((1,), (1,))
TN = ((0,), (0,))


def exact_dot(ones_mat, values):
    first = values.astype(LOW)
    rest = values - first.astype(F32)
    second = rest.astype(LOW)
    third = (rest - second.astype(F32)).astype(LOW)
    return mm(ones_mat, third) + mm(ones_mat, second) + mm(ones_mat, first)


def sigmoid(values):
    return 1.0 / (1.0 + jnp.exp(-values))


def softplus(values):
    return jnp.maximum(values, 0.0) + jnp.log1p(jnp.exp(-jnp.abs(values)))


def block_ones(rows, upper):
    row_ids = lax.broadcasted_iota(jnp.int32, (rows, rows), 0)
    col_ids = lax.broadcasted_iota(jnp.int32, (rows, rows), 1)
    same = (row_ids // SPAN) == (col_ids // SPAN)
    side = (row_ids <= col_ids) if upper else (row_ids >= col_ids)
    return jnp.where(same & side, 1.0, 0.0).astype(LOW)


def span_ids():
    return (
        lax.broadcasted_iota(jnp.int32, (SPAN, SPAN), 0),
        lax.broadcasted_iota(jnp.int32, (SPAN, SPAN), 1),
    )


def unit_lower_inverses(lowers):
    row_ids, col_ids = span_ids()
    inverses = None
    size = 1
    while size < SPAN:
        joined = (row_ids // (2 * size) == col_ids // (2 * size)) & (
            (row_ids // size) % 2 == 1
        ) & ((col_ids // size) % 2 == 0)
        parts = [jnp.where(joined, lower, 0.0) for lower in lowers]
        if inverses is None:
            eye = jnp.where(row_ids == col_ids, 1.0, 0.0)
            inverses = [eye - part for part in parts]
        else:
            halves = [mm(inverse, part) for inverse, part in zip(inverses, parts)]
            inverses = [
                inverse - mm(half, inverse) for half, inverse in zip(halves, inverses)
            ]
        size *= 2
    return inverses


class Columns:
    def __init__(self, head_count):
        self.q = 0
        self.k = head_count * DK
        self.v = 2 * head_count * DK
        self.o = self.v + head_count * DV
        self.ab = self.o + head_count * DV
        self.width = self.ab + LANES


def gates(ab_rows, par_ref, rows, head_count):
    shifted = ab_rows + par_ref[0:1, :]
    log_decay = -jnp.exp(par_ref[1:2, :]) * softplus(shifted)
    lane = lax.broadcasted_iota(jnp.int32, (rows, LANES), 1)
    log_decay = jnp.where(lane < head_count, log_decay, 0.0)
    cumulative = exact_dot(block_ones(rows, False), log_decay)
    beta = sigmoid(ab_rows)
    return shifted, log_decay, cumulative, beta


def conv_rows(padded, taps, start, cols):
    first = 8 - (CONV - 1) + start
    total = padded[first : first + SPAN, cols] * taps[0:1, :]
    for offset in range(1, CONV):
        total = total + padded[first + offset : first + offset + SPAN, cols] * taps[
            offset : offset + 1, :
        ]
    return total


def pair_inputs(head, block, cols, padded, taps_q, taps_k, taps_v, scal):
    cumulative, cum_t, beta, grow, fade = scal
    start = block * SPAN
    rows = slice(start, start + SPAN)
    qs = slice(cols.q + head * DK, cols.q + (head + 1) * DK)
    ks = slice(cols.k + head * DK, cols.k + (head + 1) * DK)
    vs = slice(cols.v + head * DV, cols.v + (head + 1) * DV)
    hk = slice(head * DK, (head + 1) * DK)
    hv = slice(head * DV, (head + 1) * DV)
    sq = conv_rows(padded, taps_q[:, hk], start, qs)
    sk = conv_rows(padded, taps_k[:, hk], start, ks)
    sv = conv_rows(padded, taps_v[:, hv], start, vs)
    gq, gk, gv = sigmoid(sq), sigmoid(sk), sigmoid(sv)
    cq, ck, cv = sq * gq, sk * gk, sv * gv
    rq = lax.rsqrt(jnp.sum(cq * cq, -1, keepdims=True) + 1e-06)
    rk = lax.rsqrt(jnp.sum(ck * ck, -1, keepdims=True) + 1e-06)
    unit_q = cq * rq
    key = ck * rk
    query = unit_q * DK ** (-0.5)
    cum_col = cumulative[rows, head : head + 1]
    cum_row = cum_t[head : head + 1, rows]
    row_ids, col_ids = span_ids()
    causal = row_ids >= col_ids
    decays = jnp.where(causal, jnp.exp(jnp.where(causal, cum_col - cum_row, 0.0)), 0.0)
    beta_col = beta[rows, head_lane(head, taps_q) : head_lane(head, taps_q) + 1]
    grow_col = grow[rows, head : head + 1]
    fade_col = fade[rows, head : head + 1]
    return dict(
        sq=sq, sk=sk, sv=sv, gq=gq, gk=gk, gv=gv, rq=rq, rk=rk, unit_q=unit_q, key=key,
        query=query, value=cv, decays=decays, beta=beta_col, grow=grow_col, fade=fade_col,
        strict=row_ids > col_ids,
    )


def head_lane(head, taps_q):
    return taps_q.shape[1] // DK + head


def chunk_scalars(ab_rows, par_ref, rows, head_count):
    shifted, log_decay, cumulative, beta = gates(ab_rows, par_ref, rows, head_count)
    cum_t = cumulative.T
    grow = jnp.exp(cumulative)
    fades = []
    ends = []
    for block in range(rows // SPAN):
        last = cumulative[(block + 1) * SPAN - 1 : (block + 1) * SPAN, :]
        fades.append(jnp.exp(last - cumulative[block * SPAN : (block + 1) * SPAN, :]))
        ends.append(jnp.exp(last))
    fade = jnp.concatenate(fades, 0) if len(fades) > 1 else fades[0]
    return shifted, log_decay, (cumulative, cum_t, beta, grow, fade), ends


def forward_kernel(
    head_count, rows, rank_ref, pre_ref, tq_ref, tk_ref, tv_ref, par_ref, gain_ref,
    mixed_ref, core_ref, state_ref, newv_ref, inv_ref, wrow_ref, carried, padded,
):
    cols = Columns(head_count)
    blocks = rows // SPAN
    conv_width = cols.o

    @pl.when(pl.program_id(1) == 0)
    def _():
        carried[...] = jnp.zeros_like(carried)
        padded[0:8, :] = jnp.zeros((8, conv_width), F32)

    @pl.when(pl.program_id(1) > 0)
    def _():
        padded[0:8, :] = padded[rows : rows + 8, :]

    padded[8 : 8 + rows, :] = pre_ref[:, 0:conv_width]
    _, _, scal, ends = chunk_scalars(
        pre_ref[:, cols.ab : cols.ab + LANES], par_ref, rows, head_count
    )
    taps = (tq_ref[...], tk_ref[...], tv_ref[...])
    pairs = [(block, head) for block in range(blocks) for head in range(head_count)]
    inputs, inners, lowers = [], [], []
    for block, head in pairs:
        got = pair_inputs(head, block, cols, padded, *taps, scal)
        both = jnp.concatenate([got["query"].astype(LOW), got["key"].astype(LOW)], 0)
        products = mm(both, got["key"], NT)
        inners.append((products[0:SPAN] * got["decays"]).astype(LOW))
        lowers.append(
            jnp.where(got["strict"], products[SPAN:] * got["decays"] * got["beta"], 0.0)
        )
        scaled = jnp.concatenate(
            [
                (got["beta"] * got["grow"] * got["key"]).astype(LOW),
                (got["beta"] * got["value"]).astype(LOW),
            ],
            1,
        )
        inputs.append(
            (
                scaled,
                (got["grow"] * got["query"]).astype(LOW),
                (got["fade"] * got["key"]).astype(LOW),
            )
        )
    ready = {}
    for (block, head), inverse, (scaled, read, faded), inner in zip(
        pairs, unit_lower_inverses(lowers), inputs, inners
    ):
        span = slice(block * SPAN, (block + 1) * SPAN)
        inverse = inverse.astype(LOW)
        inv_ref[span, head * SPAN : (head + 1) * SPAN] = inverse
        solved = mm(inverse, scaled)
        w_rows = solved[:, 0:DK].astype(LOW)
        wrow_ref[span, head * DK : (head + 1) * DK] = w_rows
        ready[block, head] = (
            jnp.concatenate([read, w_rows], 0), solved[:, DK:], inner, faded
        )
    states = [carried[head] for head in range(head_count)]
    for block in range(blocks):
        for head in range(head_count):
            state = states[head]
            sides, u_rows, inner, faded = ready[block, head]
            span = slice(block * SPAN, (block + 1) * SPAN)
            hv = slice(head * DV, (head + 1) * DV)
            low_state = state.astype(LOW)
            state_ref[0, block, head] = low_state
            read = mm(sides, low_state)
            new_values = (u_rows - read[SPAN:]).astype(LOW)
            newv_ref[span, hv] = new_values
            states[head] = ends[block][0:1, head : head + 1] * state + mm(faded, new_values, TN)
            core = read[0:SPAN] + mm(inner, new_values)
            core_ref[span, hv] = core.astype(LOW)
            gate = pre_ref[span, cols.o + head * DV : cols.o + (head + 1) * DV]
            scale = lax.rsqrt(jnp.mean(core * core, -1, keepdims=True) + 1e-05)
            mixed_ref[span, hv] = (
                core * scale * gain_ref[...] * (gate * sigmoid(gate))
            ).astype(LOW)
    for head in range(head_count):
        carried[head] = states[head]


def mixer_forward(pre, taps_q, taps_k, taps_v, params, gain, rank, head_count, rows=256):
    cols = Columns(head_count)
    tokens = pre.shape[0]
    seqs = tokens // SEQ_LEN
    chunks = SEQ_LEN // rows
    blocks = rows // SPAN
    kw, vw = head_count * DK, head_count * DV
    at = lambda s, c, rk: (s * chunks + (c ^ rk[1]), 0)
    spec = pltpu.PrefetchScalarGridSpec(
        num_scalar_prefetch=1,
        grid=(seqs, chunks),
        in_specs=[
            pl.BlockSpec((rows, cols.width), at),
            pl.BlockSpec((CONV, kw), lambda s, c, rk: (0, rk[0])),
            pl.BlockSpec((CONV, kw), lambda s, c, rk: (0, rk[0])),
            pl.BlockSpec((CONV, vw), lambda s, c, rk: (0, rk[0])),
            pl.BlockSpec((8, LANES), lambda s, c, rk: (0, 0)),
            pl.BlockSpec((1, DV), lambda s, c, rk: (0, 0)),
        ],
        out_specs=[
            pl.BlockSpec((rows, vw), at),
            pl.BlockSpec((rows, vw), at),
            pl.BlockSpec((1, blocks, head_count, DK, DV), lambda s, c, rk: (s, c, 0, 0, 0)),
            pl.BlockSpec((rows, vw), at),
            pl.BlockSpec((rows, head_count * SPAN), at),
            pl.BlockSpec((rows, kw), at),
        ],
        scratch_shapes=[
            pltpu.VMEM((head_count, DK, DV), F32),
            pltpu.VMEM((rows + 8, cols.o), F32),
        ],
    )
    shape = jax.ShapeDtypeStruct
    return pl.pallas_call(
        functools.partial(forward_kernel, head_count, rows),
        grid_spec=spec,
        out_shape=[
            shape((tokens, vw), LOW),
            shape((tokens, vw), LOW),
            shape((seqs, SEQ_LEN // SPAN, head_count, DK, DV), LOW),
            shape((tokens, vw), LOW),
            shape((tokens, head_count * SPAN), LOW),
            shape((tokens, kw), LOW),
        ],
        compiler_params=pltpu.CompilerParams(
            dimension_semantics=("arbitrary", "arbitrary"), vmem_limit_bytes=48 * 1024 * 1024
        ),
        name="mixer_forward",
    )(rank, pre, taps_q, taps_k, taps_v, params, gain)


def backward_kernel(
    head_count, rows, rank_ref, pre_ref, prev_ref, tq_ref, tk_ref, tv_ref, par_ref, gain_ref,
    dmix_ref, core_ref, state_ref, newv_ref, inv_ref, wrow_ref,
    dpre_ref, dtaps_ref, dpar_ref, dgain_ref, carried, padded, dconv,
):
    cols = Columns(head_count)
    blocks = rows // SPAN
    conv_width = cols.o
    chunk = pl.num_programs(1) - 1 - pl.program_id(1)

    @pl.when((pl.program_id(0) == 0) & (pl.program_id(1) == 0))
    def _():
        dtaps_ref[...] = jnp.zeros_like(dtaps_ref)
        dpar_ref[...] = jnp.zeros_like(dpar_ref)
        dgain_ref[...] = jnp.zeros_like(dgain_ref)

    @pl.when(pl.program_id(1) == 0)
    def _():
        carried[...] = jnp.zeros_like(carried)
        dconv[rows : rows + 8, :] = jnp.zeros((8, conv_width), F32)

    @pl.when(pl.program_id(1) > 0)
    def _():
        dconv[rows : rows + 8, :] = dconv[0:8, :]

    padded[0:8, :] = jnp.where(chunk > 0, prev_ref[:, 0:conv_width], 0.0)
    padded[8 : 8 + rows, :] = pre_ref[:, 0:conv_width]
    shifted, log_decay, scal, ends = chunk_scalars(
        pre_ref[:, cols.ab : cols.ab + LANES], par_ref, rows, head_count
    )
    beta_all = scal[2]
    taps = (tq_ref[...], tk_ref[...], tv_ref[...])
    row_ids, col_ids = span_ids()
    upper_ones = jnp.where(row_ids <= col_ids, 1.0, 0.0).astype(LOW)
    gain = gain_ref[...]
    dgain = jnp.zeros((1, DV), F32)
    ready = {}
    for block in range(blocks):
        span = slice(block * SPAN, (block + 1) * SPAN)
        for head in range(head_count):
            hv = slice(head * DV, (head + 1) * DV)
            got = pair_inputs(head, block, cols, padded, *taps, scal)
            gate = pre_ref[span, cols.o + head * DV : cols.o + (head + 1) * DV]
            core = core_ref[span, hv].astype(F32)
            d_mixed = dmix_ref[span, hv].astype(F32)
            scale = lax.rsqrt(jnp.mean(core * core, -1, keepdims=True) + 1e-05)
            unit = core * scale
            sig_gate = sigmoid(gate)
            act_gate = gate * sig_gate
            with_unit = d_mixed * unit
            dgain = dgain + jnp.sum(with_unit * act_gate, 0, keepdims=True)
            dpre_ref[span, cols.o + head * DV : cols.o + (head + 1) * DV] = (
                with_unit * gain * (sig_gate + act_gate * (1.0 - sig_gate))
            ).astype(LOW)
            d_unit = d_mixed * gain * act_gate
            d_core = (
                scale * (d_unit - unit * jnp.mean(d_unit * unit, -1, keepdims=True))
            ).astype(LOW)
            query, key = got["query"].astype(LOW), got["key"].astype(LOW)
            both = jnp.concatenate([query, key], 0)
            products = mm(both, key, NT)
            got["inner"] = products[0:SPAN] * got["decays"]
            got["kk"] = jnp.where(got["strict"], products[SPAN:] * got["decays"], 0.0)
            got["both"] = both
            got["read"] = got["grow"] * got["query"]
            got["faded"] = got["fade"] * got["key"]
            got["d_core"] = d_core
            got["from_read"] = mm(got["read"], d_core, TN)
            got["from_inner"] = mm(got["inner"], d_core, TN)
            ready[block, head] = got
    dgain_ref[...] += dgain
    d_states = [carried[head] for head in range(head_count)]
    for block in reversed(range(blocks)):
        for head in range(head_count):
            d_state = d_states[head]
            span = slice(block * SPAN, (block + 1) * SPAN)
            hv = slice(head * DV, (head + 1) * DV)
            got = ready[block, head]
            low_d = d_state.astype(LOW)
            d_new = (got["from_inner"] + mm(got["faded"], low_d)).astype(LOW)
            w_rows = wrow_ref[span, head * DK : (head + 1) * DK]
            end = ends[block][0:1, head : head + 1]
            got["d_faded"] = mm(newv_ref[span, hv], low_d, NT)
            kept = end * d_state
            got["d_end"] = jnp.sum(
                jnp.sum(kept * state_ref[0, block, head].astype(F32), 0, keepdims=True),
                1,
                keepdims=True,
            )
            d_states[head] = got["from_read"] - mm(w_rows, d_new, TN) + kept
            got["d_new"] = d_new
    for head in range(head_count):
        carried[head] = d_states[head]
    lane = lax.broadcasted_iota(jnp.int32, (SPAN, LANES), 1)
    d_cums, d_betas = [], []
    for block in range(blocks):
        span = slice(block * SPAN, (block + 1) * SPAN)
        summed = jnp.zeros((SPAN, LANES), F32)
        direct = jnp.zeros((SPAN, LANES), F32)
        d_beta_all = jnp.zeros((SPAN, LANES), F32)
        for head in range(head_count):
            got = ready[block, head]
            hv = slice(head * DV, (head + 1) * DV)
            inverse = inv_ref[span, head * SPAN : (head + 1) * SPAN]
            solved = mm(inverse, got["d_new"], TN)
            left = jnp.concatenate([got["d_core"], solved.astype(LOW)], 0)
            right = jnp.concatenate([state_ref[0, block, head], newv_ref[span, hv]], 0)
            wide = mm(left, right, NT)
            d_read, d_inner = wide[0:SPAN, 0:DK], wide[0:SPAN, DK:]
            d_wk = -wide[SPAN:, 0:DK]
            d_lower = jnp.where(got["strict"], -wide[SPAN:, DK:], 0.0)
            beta, grow, fade, key = got["beta"], got["grow"], got["fade"], got["key"]
            grown = grow * key
            with_grown = jnp.sum(d_wk * grown, -1, keepdims=True)
            lower_kk = d_lower * got["kk"]
            crossing = beta * lower_kk + d_inner * got["inner"]
            tails = jnp.where(got["strict"], mm(upper_ones, crossing), 0.0)
            faded_sum = jnp.sum(got["d_faded"] * got["faded"], -1, keepdims=True)
            point = (
                jnp.sum(d_read * got["read"], -1, keepdims=True)
                - faded_sum
                + beta * with_grown
            )
            whole = (
                jnp.sum(tails, -1, keepdims=True)
                + got["d_end"]
                + jnp.sum(faded_sum, 0, keepdims=True)
            )
            d_beta = (
                with_grown
                + jnp.sum(solved * got["value"], -1, keepdims=True)
                + jnp.sum(lower_kk, -1, keepdims=True)
            )
            summed = jnp.where(lane == head, point, summed)
            direct = jnp.where(lane == head, whole, direct)
            d_beta_all = jnp.where(lane == head_count + head, d_beta, d_beta_all)
            d_qk = d_inner * got["decays"]
            d_kk = d_lower * got["decays"] * beta
            d_both = jnp.concatenate([d_qk.astype(LOW), d_kk.astype(LOW)], 0)
            forward_part = mm(d_both, got["both"][SPAN:])
            d_query = grow * d_read + forward_part[0:SPAN]
            d_key = (
                fade * got["d_faded"]
                + beta * grow * d_wk
                + forward_part[SPAN:]
                + mm(d_both, got["both"], TN)
            )
            d_unit_q = d_query * DK ** (-0.5)
            unit_q = got["unit_q"]
            d_cq = got["rq"] * (
                d_unit_q - unit_q * jnp.sum(d_unit_q * unit_q, -1, keepdims=True)
            )
            d_ck = got["rk"] * (d_key - key * jnp.sum(d_key * key, -1, keepdims=True))
            d_cv = beta * solved
            for d_act, pre_act, sig, first, size in (
                (d_cq, got["sq"], got["gq"], cols.q + head * DK, DK),
                (d_ck, got["sk"], got["gk"], cols.k + head * DK, DK),
                (d_cv, got["sv"], got["gv"], cols.v + head * DV, DV),
            ):
                dconv[span, first : first + size] = d_act * sig * (1.0 + pre_act * (1.0 - sig))
        d_cums.append((summed, direct))
        d_betas.append(d_beta_all)
    join = lambda parts: jnp.concatenate(parts, 0) if len(parts) > 1 else parts[0]
    d_log = exact_dot(block_ones(rows, True), join([p[0] for p in d_cums])) + join(
        [p[1] for p in d_cums]
    )
    lanes_all = lax.broadcasted_iota(jnp.int32, (rows, LANES), 1)
    d_a = jnp.where(
        lanes_all < head_count, d_log * -jnp.exp(par_ref[1:2, :]) * sigmoid(shifted), 0.0
    )
    d_b = join(d_betas) * beta_all * (1.0 - beta_all)
    dpre_ref[:, cols.ab : cols.ab + LANES] = (d_a + d_b).astype(LOW)
    dpar_ref[0:1, :] += jnp.sum(d_a, 0, keepdims=True)
    dpar_ref[1:2, :] += jnp.sum(d_log * log_decay, 0, keepdims=True)
    for taps_now, base in ((taps[0], cols.q), (taps[1], cols.k), (taps[2], cols.v)):
        width = taps_now.shape[1]
        for part in range(width // LANES):
            col = slice(base + part * LANES, base + (part + 1) * LANES)
            for block in range(blocks):
                start = block * SPAN
                total = None
                now = dconv[start : start + SPAN, col]
                for tap in range(CONV):
                    ahead = start + CONV - 1 - tap
                    tap_row = taps_now[tap : tap + 1, part * LANES : (part + 1) * LANES]
                    term = (now if tap == CONV - 1 else dconv[ahead : ahead + SPAN, col]) * tap_row
                    total = term if total is None else total + term
                    behind = 8 - (CONV - 1) + tap + start
                    dtaps_ref[tap : tap + 1, col] += jnp.sum(
                        now * padded[behind : behind + SPAN, col], 0, keepdims=True
                    )
                dpre_ref[start : start + SPAN, col] = total.astype(LOW)


def mixer_backward(pre, taps_q, taps_k, taps_v, params, gain, rank, d_mixed, saved, head_count,
                   rows=256):
    cols = Columns(head_count)
    tokens = pre.shape[0]
    seqs = tokens // SEQ_LEN
    chunks = SEQ_LEN // rows
    blocks = rows // SPAN
    kw, vw = head_count * DK, head_count * DV
    at = lambda s, c, rk: (s * chunks + ((chunks - 1 - c) ^ rk[1]), 0)
    before = lambda s, c, rk: (
        (s * chunks + (jnp.maximum(chunks - 2 - c, 0) ^ rk[1]) + 1) * (rows // 8) - 1, 0)
    fixed = lambda s, c, rk: (0, 0)
    spec = pltpu.PrefetchScalarGridSpec(
        num_scalar_prefetch=1,
        grid=(seqs, chunks),
        in_specs=[
            pl.BlockSpec((rows, cols.width), at),
            pl.BlockSpec((8, cols.width), before),
            pl.BlockSpec((CONV, kw), lambda s, c, rk: (0, rk[0])),
            pl.BlockSpec((CONV, kw), lambda s, c, rk: (0, rk[0])),
            pl.BlockSpec((CONV, vw), lambda s, c, rk: (0, rk[0])),
            pl.BlockSpec((8, LANES), fixed),
            pl.BlockSpec((1, DV), fixed),
            pl.BlockSpec((rows, vw), at),
            pl.BlockSpec((rows, vw), at),
            pl.BlockSpec((1, blocks, head_count, DK, DV),
                         lambda s, c, rk: (s, chunks - 1 - c, 0, 0, 0)),
            pl.BlockSpec((rows, vw), at),
            pl.BlockSpec((rows, head_count * SPAN), at),
            pl.BlockSpec((rows, kw), at),
        ],
        out_specs=[
            pl.BlockSpec((rows, cols.width), at),
            pl.BlockSpec((CONV, cols.o), fixed),
            pl.BlockSpec((8, LANES), fixed),
            pl.BlockSpec((1, DV), fixed),
        ],
        scratch_shapes=[
            pltpu.VMEM((head_count, DK, DV), F32),
            pltpu.VMEM((rows + 8, cols.o), F32),
            pltpu.VMEM((rows + 8, cols.o), F32),
        ],
    )
    shape = jax.ShapeDtypeStruct
    return pl.pallas_call(
        functools.partial(backward_kernel, head_count, rows),
        grid_spec=spec,
        out_shape=[
            shape((tokens, cols.width), LOW),
            shape((CONV, cols.o), F32),
            shape((8, LANES), F32),
            shape((1, DV), F32),
        ],
        compiler_params=pltpu.CompilerParams(
            dimension_semantics=("arbitrary", "arbitrary"), vmem_limit_bytes=48 * 1024 * 1024
        ),
        name="mixer_backward",
    )(rank, pre, pre, taps_q, taps_k, taps_v, params, gain, d_mixed, *saved)


def rms_norm(values, gain):
    return values * lax.rsqrt(jnp.mean(values * values, -1, keepdims=True) + 1e-05) * gain


def swiglu_act(gate_val, up_val):
    return jax.nn.silu(gate_val) * up_val


def matmul_tn(left, right):
    return lax.dot_general(left, right, (TN, ((), ())), preferred_element_type=F32)


def matmul_nt(left, right):
    return lax.dot_general(left, right, (NT, ((), ())), preferred_element_type=F32)


def place_cols(member, width, offset):
    blank = jnp.zeros(member.shape[:-1] + (width,), F32)
    return lax.dynamic_update_slice_in_dim(blank, member, offset, member.ndim - 1)


def head_params(a_log, dt_bias, rank, head_count):
    slab = jnp.zeros((8, LANES), F32)
    bias = lax.dynamic_slice_in_dim(dt_bias, rank * head_count, head_count, 0)
    scale = lax.dynamic_slice_in_dim(a_log, rank * head_count, head_count, 0)
    slab = lax.dynamic_update_slice(slab, bias[None, :], (0, 0))
    return lax.dynamic_update_slice(slab, scale[None, :], (1, 0))


def join_mixer_weights(w_query, w_key, w_value, w_gate_out, w_decay, w_beta):
    blank = jnp.zeros((w_query.shape[0], LANES - 2 * w_decay.shape[1]), LOW)
    return jnp.concatenate(
        [w_query, w_key, w_value, w_gate_out, w_decay, w_beta, blank], axis=1
    )


def local_general(
    tokens, cotangent, gain_attn, gain_ffn, w_query, w_key, w_value, w_gate_out, w_decay,
    w_beta, w_output, w_ffn_gate, w_ffn_up, w_ffn_down, conv_query, conv_key, conv_value,
    a_log, dt_bias, out_gain,
):
    rank = lax.axis_index("tensor")
    head_count = w_decay.shape[1]
    cols = Columns(head_count)
    gather_rows = lambda value: lax.all_gather(value, "dp", axis=0, tiled=True)
    gather_cols = lambda value: lax.all_gather(value, "dp", axis=1, tiled=True)
    gather_tokens = lambda value: lax.all_gather(value, "tensor", axis=0, tiled=True)
    mixer_weights = gather_rows(
        join_mixer_weights(w_query, w_key, w_value, w_gate_out, w_decay, w_beta)
    )
    output_weights = gather_cols(w_output)
    gate_weights, up_weights = gather_rows(w_ffn_gate), gather_rows(w_ffn_up)
    down_weights = gather_cols(w_ffn_down)

    def scatter_tokens(value):
        return lax.psum_scatter(
            value.astype(LOW), "tensor", scatter_dimension=0, tiled=True
        ).astype(F32)

    tok_rows = tokens.astype(F32)
    normed_one, norm_one_pull = jax.vjp(rms_norm, tok_rows, gain_attn)
    mixer_in = gather_tokens(normed_one.astype(LOW))
    pre = jnp.dot(mixer_in, mixer_weights, preferred_element_type=F32)
    kernel_args = (
        pre, conv_query, conv_key, conv_value,
        head_params(a_log, dt_bias, rank, head_count), out_gain.reshape(1, DV),
        jnp.stack([rank, jnp.zeros_like(rank)]).astype(jnp.int32),
    )
    mixed, *saved = mixer_forward(*kernel_args, head_count)
    middle = tok_rows + scatter_tokens(
        jnp.dot(mixed, output_weights, preferred_element_type=F32)
    )
    normed_two, norm_two_pull = jax.vjp(rms_norm, middle, gain_ffn)
    ffn_in = gather_tokens(normed_two.astype(LOW))
    gate_val = jnp.dot(ffn_in, gate_weights, preferred_element_type=F32)
    up_val = jnp.dot(ffn_in, up_weights, preferred_element_type=F32)
    activated, swiglu_pull = jax.vjp(swiglu_act, gate_val, up_val)
    activated_low = activated.astype(LOW)
    output = (
        middle
        + scatter_tokens(jnp.dot(activated_low, down_weights, preferred_element_type=F32))
    ).astype(LOW)
    cot_rows = gather_tokens(cotangent)
    d_gate, d_up = swiglu_pull(matmul_nt(cot_rows, down_weights))
    d_gate, d_up = d_gate.astype(LOW), d_up.astype(LOW)
    grad_down = matmul_tn(activated_low, cot_rows)
    grad_gate, grad_up = matmul_tn(ffn_in, d_gate), matmul_tn(ffn_in, d_up)
    d_normed_two = scatter_tokens(
        matmul_nt(d_gate, gate_weights) + matmul_nt(d_up, up_weights)
    )
    d_middle_norm, d_gain_ffn = norm_two_pull(d_normed_two)
    d_middle = cotangent.astype(F32) + d_middle_norm
    branch_cot = gather_tokens(d_middle.astype(LOW))
    d_mixed = matmul_nt(branch_cot, output_weights).astype(LOW)
    grad_out = matmul_tn(mixed, branch_cot)
    d_pre, d_taps, d_heads, d_out_gain = mixer_backward(*kernel_args, d_mixed, saved, head_count)
    grad_mixer = matmul_tn(mixer_in, d_pre)
    d_normed_one = scatter_tokens(matmul_nt(d_pre, mixer_weights))
    d_tok_norm, d_gain_attn = norm_one_pull(d_normed_one)
    grad_tokens = d_middle + d_tok_norm

    def scatter_grad(value, dim):
        return lax.psum_scatter(
            value.astype(LOW), "dp", scatter_dimension=dim, tiled=True
        ).astype(F32)

    own_mixer = scatter_grad(grad_mixer, 0)
    edge = cols.ab + head_count
    small_sums = lax.psum(
        (
            d_gain_attn,
            d_gain_ffn,
            place_cols(d_taps[:, : cols.k], conv_query.shape[1], rank * cols.k),
            place_cols(d_taps[:, cols.k : cols.v], conv_key.shape[1], rank * cols.k),
            place_cols(d_taps[:, cols.v :], conv_value.shape[1], rank * (cols.o - cols.v)),
            place_cols(d_heads[1, :head_count], a_log.shape[0], rank * head_count),
            place_cols(d_heads[0, :head_count], dt_bias.shape[0], rank * head_count),
            d_out_gain[0],
        ),
        ("dp", "tensor"),
    )
    return (
        output, grad_tokens, small_sums[0], small_sums[1],
        own_mixer[:, : cols.k], own_mixer[:, cols.k : cols.v], own_mixer[:, cols.v : cols.o],
        own_mixer[:, cols.o : cols.ab], own_mixer[:, cols.ab : edge],
        own_mixer[:, edge : edge + head_count],
        scatter_grad(grad_out, 1), scatter_grad(grad_gate, 0), scatter_grad(grad_up, 0),
        scatter_grad(grad_down, 1), *small_sums[2:],
    )


def local_paired(
    tokens, cotangent, gain_attn, gain_ffn, w_query, w_key, w_value, w_gate_out, w_decay,
    w_beta, w_output, w_ffn_gate, w_ffn_up, w_ffn_down, conv_query, conv_key, conv_value,
    a_log, dt_bias, out_gain,
):
    n_tensor = 4
    where_dp, z = lax.axis_index("dp"), lax.axis_index("tensor")
    core, group = where_dp % 2, z // 2
    home = core == group
    own_quarter = z ^ (2 * (core ^ group))
    rank = z ^ (2 * core)
    head_count = w_decay.shape[1]
    cols = Columns(head_count)
    quarter, width = tokens.shape
    chunk = width // 4

    def send(value, move):
        routes = []
        for source in range(8):
            for plane in range(n_tensor):
                target = move(source, plane)
                if target is not None:
                    routes.append((source * n_tensor + plane, target[0] * n_tensor + target[1]))
        return lax.ppermute(value, ("dp", "tensor"), routes)

    by_core = lambda value: send(value, lambda d, p: (d ^ 1, p))
    by_x = lambda value: send(value, lambda d, p: (d ^ 2, p))
    by_y = lambda value: send(value, lambda d, p: (d ^ 4, p))
    by_pair = lambda value: send(value, lambda d, p: (d, p ^ 1))
    by_far = lambda value: send(value, lambda d, p: (d, p ^ 2))

    def to_group(value, sent=None):
        moved = send(
            value.astype(sent or value.dtype),
            lambda d, p: (d ^ 1, p ^ 2) if d % 2 != p // 2 else None,
        )
        return jnp.where(home, value, moved.astype(value.dtype))

    x_odd, y_odd = (where_dp // 2) % 2 == 1, where_dp // 4 == 1

    def reorder(value):
        parts = [value[..., index * chunk : (index + 1) * chunk] for index in range(4)]
        parts = [jnp.where(x_odd, parts[index ^ 1], parts[index]) for index in range(4)]
        parts = [jnp.where(y_odd, parts[index ^ 2], parts[index]) for index in range(4)]
        return jnp.concatenate(parts, -1)

    def gather_group(value):
        beside = by_pair(value)
        across = by_core(value)
        return jnp.concatenate([value, beside, across, by_core(beside)], 0)

    def reduce_group(make):
        far = make(slice(2 * quarter, 4 * quarter)).astype(LOW)
        moved = by_core(far)
        near = make(slice(0, 2 * quarter)) + moved.astype(F32)
        beside = by_pair(near[quarter:].astype(LOW))
        return near[:quarter] + beside.astype(F32)

    def gather_weights(shard):
        first = send(shard, lambda d, p: (d ^ 1, p) if d % 2 else (d ^ 1, p ^ 2))
        second = send(shard, lambda d, p: (d, p ^ 2) if d % 2 else None)
        held = jnp.concatenate(
            [jnp.where(core == 0, shard, first), jnp.where(core == 0, first, second)], 0
        )
        half = shard.shape[0]
        from_x, from_y = by_x(held), by_y(held)
        diagonal = [by_x(from_y[:half]), by_y(from_x[half:])]
        return [held, from_x, from_y, *diagonal]

    def scatter_weights(grad):
        grad = grad.astype(LOW)
        half = grad.shape[0] // 8
        part = lambda index: grad[2 * half * index : 2 * half * (index + 1)]
        last = part(3)
        from_x, from_y = by_x(last[:half]), by_y(last[half:])
        add = lambda left, right: (left.astype(F32) + right.astype(F32)).astype(LOW)
        to_y = jnp.concatenate([add(part(2)[:half], from_x), part(2)[half:]], 0)
        to_x = jnp.concatenate([part(1)[:half], add(part(1)[half:], from_y)], 0)
        total = (
            part(0).astype(F32) + by_x(to_x).astype(F32) + by_y(to_y).astype(F32)
        ).astype(LOW)
        first = send(
            jnp.where(core == 0, total[half:], total[:half]),
            lambda d, p: (d ^ 1, p ^ 2) if d % 2 else (d ^ 1, p),
        )
        second = send(total[half:], lambda d, p: (d, p ^ 2) if d % 2 else None)
        return first.astype(F32) + jnp.where(core == 0, total[:half], second).astype(F32)

    def column_part(pieces, first, size):
        return jnp.concatenate([piece[:, first : first + size] for piece in pieces], 0)

    units = w_ffn_gate.shape[1]
    mixer_pieces = gather_weights(
        join_mixer_weights(w_query, w_key, w_value, w_gate_out, w_decay, w_beta)
    )
    mixer_weights = jnp.concatenate(mixer_pieces, 0)
    down_end = -(-3 * units // LANES) * LANES
    other_pieces = gather_weights(
        jnp.concatenate(
            [
                w_ffn_gate, w_ffn_up, w_ffn_down.T,
                jnp.zeros((w_ffn_gate.shape[0], down_end - 3 * units), LOW), w_output.T,
            ],
            1,
        )
    )
    pair_weights = column_part(other_pieces, 0, 2 * units)
    down_weights = column_part(other_pieces, 2 * units, units)
    output_weights = column_part(other_pieces, down_end, w_output.shape[0])

    gain_one, gain_two = reorder(gain_attn)[None, :], reorder(gain_ffn)[None, :]
    tok_rows = reorder(to_group(tokens)).astype(F32)
    cot_low = reorder(to_group(cotangent))
    inverse_one = lax.rsqrt(jnp.mean(tok_rows * tok_rows, -1, keepdims=True) + 1e-05)
    mixer_in = gather_group((tok_rows * inverse_one * gain_one).astype(LOW))
    pre = jnp.dot(mixer_in, mixer_weights, preferred_element_type=F32)
    kernel_args = (
        pre, conv_query, conv_key, conv_value,
        head_params(a_log, dt_bias, rank, head_count), out_gain.reshape(1, DV),
        jnp.stack([rank, own_quarter]).astype(jnp.int32),
    )
    mixed, *saved = mixer_forward(*kernel_args, head_count, rows=quarter)
    middle = tok_rows + reduce_group(lambda rows: matmul_nt(mixed[rows], output_weights))
    inverse_two = lax.rsqrt(jnp.mean(middle * middle, -1, keepdims=True) + 1e-05)
    ffn_in = gather_group((middle * inverse_two * gain_two).astype(LOW))
    both_val = jnp.dot(ffn_in, pair_weights, preferred_element_type=F32)
    gate_val, up_val = both_val[:, :units], both_val[:, units:]
    gate_sig = jax.nn.sigmoid(gate_val)
    gate_act = gate_val * gate_sig
    activated = (gate_act * up_val).astype(LOW)
    output = middle + reduce_group(lambda rows: matmul_nt(activated[rows], down_weights))
    output = to_group(reorder(output.astype(LOW)))

    cot_rows = gather_group(cot_low)
    d_activated = jnp.dot(cot_rows, down_weights, preferred_element_type=F32)
    d_gate = d_activated * up_val * gate_sig * (1.0 + gate_val * (1.0 - gate_sig))
    d_both = jnp.concatenate([d_gate.astype(LOW), (d_activated * gate_act).astype(LOW)], 1)
    d_two = reduce_group(lambda rows: matmul_nt(d_both[rows], pair_weights))
    grad_pair = scatter_weights(matmul_tn(ffn_in, d_both))
    grad_down = scatter_weights(matmul_tn(cot_rows, activated))

    def norm_back(d_normed, values, inverse, gain):
        scaled = d_normed * gain
        unit = values * inverse
        d_gain = jnp.sum(d_normed * unit, 0)
        return d_gain, inverse * (scaled - unit * jnp.mean(scaled * unit, -1, keepdims=True))

    d_gain_two, d_middle = norm_back(d_two, middle, inverse_two, gain_two)
    d_middle = cot_low.astype(F32) + d_middle
    branch_cot = gather_group(d_middle.astype(LOW))
    d_mixed = jnp.dot(branch_cot, output_weights, preferred_element_type=F32).astype(LOW)
    d_pre, d_taps, d_heads, d_out_gain = mixer_backward(
        *kernel_args, d_mixed, saved, head_count, rows=quarter
    )
    grad_out = scatter_weights(matmul_tn(branch_cot, mixed))
    grad_mixer = scatter_weights(matmul_tn(mixer_in, d_pre))
    d_one = reduce_group(lambda rows: matmul_nt(d_pre[rows], mixer_weights))
    d_gain_one, d_tokens = norm_back(d_one, tok_rows, inverse_one, gain_one)
    grad_tokens = to_group(reorder(d_middle + d_tokens), LOW)

    small = (
        reorder(d_gain_one),
        reorder(d_gain_two),
        place_cols(d_taps[:, : cols.k], conv_query.shape[1], rank * cols.k),
        place_cols(d_taps[:, cols.k : cols.v], conv_key.shape[1], rank * cols.k),
        place_cols(d_taps[:, cols.v :], conv_value.shape[1], rank * (cols.o - cols.v)),
        place_cols(d_heads[1, :head_count], a_log.shape[0], rank * head_count),
        place_cols(d_heads[0, :head_count], dt_bias.shape[0], rank * head_count),
        d_out_gain[0],
    )
    flat = jnp.concatenate([member.reshape(-1) for member in small])
    for step in (by_core, by_x, by_y, by_pair, by_far):
        flat = flat + step(flat)
    sums, first = [], 0
    for member in small:
        sums.append(flat[first : first + member.size].reshape(member.shape))
        first += member.size
    edge = cols.ab + head_count
    return (
        output, grad_tokens, sums[0], sums[1],
        grad_mixer[:, : cols.k], grad_mixer[:, cols.k : cols.v],
        grad_mixer[:, cols.v : cols.o], grad_mixer[:, cols.o : cols.ab],
        grad_mixer[:, cols.ab : edge], grad_mixer[:, edge : edge + head_count],
        grad_out.T, grad_pair[:, :units], grad_pair[:, units:], grad_down.T, *sums[2:],
    )


def solution(mesh):
    paired = mesh.shape["dp"] == 8 and mesh.shape["tensor"] == 4
    spread = P(("dp", "tensor"), None)
    rows_split, cols_split = P("dp", "tensor"), P("tensor", "dp")
    return jax.shard_map(
        local_paired if paired else local_general,
        mesh=mesh,
        in_specs=(spread, spread, P(), P())
        + (rows_split,) * 6
        + (cols_split, rows_split, rows_split, cols_split)
        + (P(),) * 6,
        out_specs=(spread, spread, P(), P())
        + (rows_split,) * 6
        + (cols_split, rows_split, rows_split, cols_split)
        + (P(),) * 6,
        check_vma=False,
    )
```
